32 devices in a mesh: rows: 2 (over x), cols: 16 (over z, y, core).
Axes of the slice: x: 2, y: 2, z: 4, core: 2. Of those that a mesh axis runs over, the one named last changes fastest.
Arguments:
- queries: bfloat16 [8192, 1024], P(('rows', 'cols')), may hold values from -1 to 1
- attn_out: bfloat16 [8192, 1024], P(('rows', 'cols')), may hold values from -6 to 6
- out_grad: bfloat16 [8192, 1024], P(('rows', 'cols')), may hold values from -96 to 96
- log_norm: float32 [8192, 8], P(('rows', 'cols')), may hold values from 7.5 to 8.5
- leaf_kv: bfloat16 [8192, 256], P(('rows', 'cols')), may hold values from -1 to 1
- root_kv: bfloat16 [2048, 256], P('cols'), may hold values from -1 to 1
- branch_kv: bfloat16 [4, 1024, 256], P('rows', 'cols'), may hold values from -1 to 1
- branch_len: int32 [4], replicated, may hold values from 256 to 1024, as said below
- segment_ids: int32 [32, 256], P(('rows', 'cols')), may hold values from 0 to 7, never falling along the last dimension, each value on 1 to 128 neighbouring positions
- segment_branch: int32 [32, 8], P(('rows', 'cols')), may hold values from 0 to 1
Outputs:
- query_grad: bfloat16 [8192, 1024], P(('rows', 'cols'))
- leaf_kv_grad: float32 [8192, 256], P(('rows', 'cols'))
- root_kv_grad: float32 [2048, 256], P('cols')
- branch_kv_grad: float32 [4, 1024, 256], P('rows', 'cols')
The draws below stay inside these ranges and needn't reach their ends.
Inputs may be any that keep to these rules, and one draw needn't show every extreme that they name: `branch_len`: every branch has between 256 and 1024 live slots; some branch has exactly 1024 and some exactly 256. `segment_ids`: never falling along a device's tokens; each segment has 1 to 128 tokens, one exactly 128. `segment_branch`: a segment on row r extends branch r * 2 + value.
All inputs are finite; a program needn't handle non-finite values.
Results may differ from the reference program's by a relative error of at most 0.0041.
Values may be sent and summed in bfloat16 or wider, within the bound.
A program may use at most 64 MiB of HBM per device.

```python
import math
import jax
import jax.numpy as jnp
import numpy as np
from jax import lax

HEADS = 8
HD = 128
TOK_DEV = 256
ROOT = 2048
BLEN = 1024
BR_DEV = 2
SEGS = 8
SEG_MAX = 128
KVW = 256
BRANCHES = 4
DEVS = 32
LEAF = 8192
N_ROWS = 2
N_COLS = 16


def draw_branch_len(key, part):
    first, second, third = jax.random.split(jax.random.fold_in(key, 71), 3)
    lengths = jax.random.randint(first, (BRANCHES,), BLEN // 4, BLEN + 1, dtype=jnp.int32)
    longest = jax.random.randint(second, (), 0, BRANCHES, dtype=jnp.int32)
    offset = jax.random.randint(third, (), 1, BRANCHES, dtype=jnp.int32)
    shortest = (longest + offset) % BRANCHES
    return lengths.at[longest].set(BLEN).at[shortest].set(BLEN // 4)


def set_ends(values, rng, least, largest):
    longest = values.shape.index(max(values.shape))
    spots = []
    for shift in (0, 1):
        where = [jax.random.randint(jax.random.fold_in(rng, axis), (), 0, length) for axis, length in enumerate(values.shape)]
        where[longest] = (where[longest] + shift) % values.shape[longest]
        spots.append(tuple(where))
    return values.at[spots[0]].set(least).at[spots[1]].set(largest)


def block_scale(stream_key, dims, cuts, low, largest):
    factor_of, own = 1.0, jax.random.fold_in(stream_key, 6)
    for position, blocks in cuts:
        draws = jnp.exp(jax.random.uniform(jax.random.fold_in(own, position), (blocks,), jnp.float32, low / len(cuts), largest / len(cuts)))
        factor_of = factor_of * jnp.repeat(draws, dims[position] // blocks).reshape([-1 if axis == position else 1 for axis in range(len(dims))])
    return factor_of


def profile(amount, total, limit, slope):
    portions = [(1 << 20) // math.isqrt(grade ** slope) + 1 for grade in range(2, amount + 1)]
    rest, counts = total - limit - (amount - 1), [1] * (amount - 1)
    while rest > 0:
        free = [i for i in range(amount - 1) if counts[i] < limit]
        mass, budget = sum([portions[i] for i in free]), rest
        for i in free:
            more = min(limit - counts[i], max(1, budget * portions[i] // mass), rest)
            counts[i] = counts[i] + more
            rest = rest - more
    return np.array([limit] + counts)


def uneven(stream_key, amount, total, reach, slope):
    if amount == 2:
        one = jax.random.randint(stream_key, (), max(1, total - reach), min(reach, total - 1) + 1)
        return jnp.stack([one, total - one])
    sizes = jnp.asarray(profile(amount, total, reach, slope), jnp.int32)
    twos = (amount - 1) // 2
    donor, taker = sizes[1:1 + 2 * twos:2], sizes[2:2 + 2 * twos:2]
    room = jnp.minimum(donor - 1, reach - taker)
    moved = jax.random.randint(jax.random.fold_in(stream_key, 1), (twos,), 0, 1 << 20) % (room + 1)
    sizes = sizes.at[1:1 + 2 * twos:2].set(donor - moved).at[2:2 + 2 * twos:2].set(taker + moved)
    return sizes[jax.random.permutation(jax.random.fold_in(stream_key, 2), amount)]


def centred(own_key, extent, deviation, most, shards=(), kind=jnp.bfloat16):
    drawn = deviation * jax.random.normal(own_key, extent, jnp.float32)
    if shards:
        drawn = drawn * block_scale(own_key, extent, shards, -0.22, 0.18)
    return jnp.clip(drawn, -most, most).astype(kind)


def setup_inputs(seed: int = 0) -> dict:
    streams_of = jax.random.split(jax.random.key(seed), 11)
    return {
        "queries": jnp.clip(jax.random.uniform(streams_of[0], (LEAF, HEADS * HD), jnp.float32, -1.0, 1.0) * block_scale(streams_of[0], (LEAF, HEADS * HD), ((0, 32),), -0.4, 0.0), -1.0, 1.0).astype(jnp.bfloat16),
        "attn_out": centred(streams_of[1], (LEAF, HEADS * HD), 1.0, 6.0, ((0, 32),)),
        "out_grad": centred(streams_of[2], (LEAF, HEADS * HD), 16.0, 96.0, ((0, 32),)),
        "log_norm": jnp.clip(7.5 + 1.0 * jax.random.uniform(streams_of[3], (LEAF, HEADS), jnp.float32) ** block_scale(streams_of[3], (LEAF, HEADS), ((0, 32),), -0.2, 0.2), 7.5, 8.5),
        "leaf_kv": jnp.clip(jax.random.uniform(streams_of[4], (LEAF, KVW), jnp.float32, -1.0, 1.0) * block_scale(streams_of[4], (LEAF, KVW), ((0, 32),), -0.4, 0.0), -1.0, 1.0).astype(jnp.bfloat16),
        "root_kv": jnp.clip(jax.random.uniform(streams_of[5], (ROOT, KVW), jnp.float32, -1.0, 1.0) * block_scale(streams_of[5], (ROOT, KVW), ((0, 16),), -0.4, 0.0), -1.0, 1.0).astype(jnp.bfloat16),
        "branch_kv": jnp.clip(jax.random.uniform(streams_of[6], (BRANCHES, BLEN, KVW), jnp.float32, -1.0, 1.0) * block_scale(streams_of[6], (BRANCHES, BLEN, KVW), ((0, 2), (1, 16)), -0.4, 0.0), -1.0, 1.0).astype(jnp.bfloat16),
        "branch_len": draw_branch_len(jax.random.fold_in(streams_of[10], 71), 0),
        "segment_ids": jax.vmap(lambda own: jnp.searchsorted(jnp.cumsum(uneven(own, SEGS, TOK_DEV, SEG_MAX, 0)), jnp.arange(TOK_DEV), side="right"))(jax.random.split(streams_of[8], DEVS)).reshape((DEVS, TOK_DEV)).astype(jnp.int32),
        "segment_branch": set_ends(jax.random.randint(streams_of[9], (DEVS, SEGS), 0, BR_DEV), jax.random.fold_in(streams_of[9], 1), 0, BR_DEV - 1).astype(jnp.int32),
    }


def block_grads(query_heads, grad_heads, log_norm, row_delta, key_rows, allowed):
    scale = HD ** -0.5
    keys_f = key_rows[:, :HD].astype(jnp.float32)
    values_f = key_rows[:, HD:].astype(jnp.float32)
    query_f = query_heads.astype(jnp.float32)
    grad_f = grad_heads.astype(jnp.float32)
    scores = jnp.einsum('thd,kd->thk', query_f, keys_f) * scale
    weights = jnp.where(allowed[:, None, :], jnp.exp(scores - log_norm[:, :, None]), 0.0)
    dweight = jnp.einsum('thd,kd->thk', grad_f, values_f)
    dscore = weights * (dweight - row_delta[:, :, None])
    weight_b = lax.optimization_barrier(weights.astype(jnp.bfloat16)).astype(jnp.float32)
    dscore_b = lax.optimization_barrier(dscore.astype(jnp.bfloat16)).astype(jnp.float32)
    query_part = jnp.einsum('thk,kd->thd', dscore_b, keys_f) * scale
    key_grad = jnp.einsum('thk,thd->kd', dscore_b, query_f) * scale
    value_grad = jnp.einsum('thk,thd->kd', weight_b, grad_f)
    return query_part, jnp.concatenate([key_grad, value_grad], axis=1)


def device_grads(queries, attn_out, out_grad, log_norm, leaf_kv, segment, seg_branch, root_kv, branch_rows, lengths):
    tokens = queries.shape[0]
    query_heads = queries.reshape(tokens, HEADS, HD)
    grad_heads = out_grad.reshape(tokens, HEADS, HD)
    out_heads = attn_out.reshape(tokens, HEADS, HD)
    row_delta = jnp.sum(grad_heads.astype(jnp.float32) * out_heads.astype(jnp.float32), axis=2)
    full = jnp.ones((tokens, root_kv.shape[0]), dtype=bool)
    query_grad, root_term = block_grads(query_heads, grad_heads, log_norm, row_delta, root_kv, full)
    token_branch = jnp.sum(jnp.where(segment[:, None] == jnp.arange(SEGS, dtype=jnp.int32)[None, :], seg_branch[None, :], 0), axis=1)
    branch_terms = []
    for slot in range(BR_DEV):
        live_slot = jnp.arange(BLEN, dtype=jnp.int32) < lengths[slot]
        allowed = (token_branch == slot)[:, None] & live_slot[None, :]
        part, term = block_grads(query_heads, grad_heads, log_norm, row_delta, branch_rows[slot], allowed)
        query_grad = query_grad + part
        branch_terms.append(term)
    positions = jnp.arange(tokens, dtype=jnp.int32)
    allowed = (segment[:, None] == segment[None, :]) & (positions[None, :] <= positions[:, None])
    part, leaf_term = block_grads(query_heads, grad_heads, log_norm, row_delta, leaf_kv, allowed)
    query_grad = query_grad + part
    return query_grad.reshape(tokens, HEADS * HD).astype(jnp.bfloat16), leaf_term, root_term, jnp.stack(branch_terms)


def reference(queries, attn_out, out_grad, log_norm, leaf_kv, root_kv, branch_kv, branch_len, segment_ids, segment_branch):
    def one_device(carry, device):
        root_acc, branch_acc = carry
        start = device * TOK_DEV

        def rows_of(array):
            return lax.dynamic_slice_in_dim(array, start, TOK_DEV, 0)

        row_start = (device // N_COLS) * BR_DEV
        branch_rows = lax.dynamic_slice_in_dim(branch_kv, row_start, BR_DEV, 0)
        lengths = lax.dynamic_slice_in_dim(branch_len, row_start, BR_DEV, 0)
        segment = lax.dynamic_index_in_dim(segment_ids, device, 0, keepdims=False)
        seg_branch = lax.dynamic_index_in_dim(segment_branch, device, 0, keepdims=False)
        query_grad, leaf_term, root_term, branch_term = device_grads(
            rows_of(queries), rows_of(attn_out), rows_of(out_grad), rows_of(log_norm), rows_of(leaf_kv),
            segment, seg_branch, root_kv, branch_rows, lengths)
        old = lax.dynamic_slice_in_dim(branch_acc, row_start, BR_DEV, 0)
        branch_acc = lax.dynamic_update_slice_in_dim(branch_acc, old + branch_term, row_start, 0)
        return (root_acc + root_term, branch_acc), (query_grad, leaf_term)

    start_carry = (jnp.zeros((ROOT, KVW), jnp.float32), jnp.zeros((BRANCHES, BLEN, KVW), jnp.float32))
    devices = jnp.arange(N_ROWS * N_COLS, dtype=jnp.int32)
    (root_grad, branch_grad), (query_grad, leaf_grad) = lax.scan(one_device, start_carry, devices)
    return (query_grad.reshape(LEAF, HEADS * HD), leaf_grad.reshape(LEAF, KVW), root_grad, branch_grad)
```

```python
import functools

import jax
import jax.numpy as jnp
from jax import lax
from jax.experimental import pallas as pl
from jax.experimental.pallas import tpu as pltpu
from jax.sharding import PartitionSpec as P

HEADS = 8
HD = 128
KB = 256
MESH = pl.DeviceIdType.MESH
F32 = jnp.float32
BF16 = jnp.bfloat16
LOG2E = 1.4426950408889634
VMEM = pl.BlockSpec(memory_space=pltpu.VMEM)
SMEM = pl.BlockSpec(memory_space=pltpu.SMEM)


def split_cols(cols):
    core = 2 if cols % 2 == 0 else 1
    chips = cols // core
    outer = 4 if chips % 4 == 0 else chips
    return outer, chips // outer, core


class Place:
    def __init__(self, cols):
        self.O, self.I, self.C = split_cols(cols)
        self.row = lax.axis_index("rows")
        me = lax.axis_index("cols")
        self.c = lax.rem(me, self.C)
        chip = me // self.C
        self.y = lax.rem(chip, self.I)
        self.z = chip // self.I

    def index(self, dz, dy, dc):
        z = lax.rem(self.z + dz + self.O, self.O)
        y = lax.rem(self.y + dy + self.I, self.I)
        c = lax.rem(self.c + dc + self.C, self.C)
        return (z * self.I + y) * self.C + c

    def dev(self, dz, dy, dc):
        return (self.row, self.index(dz, dy, dc))

    def greet(self, rows=1):
        sem = pltpu.get_barrier_semaphore()
        peers = [self.dev(d, 0, 0) for d in range(1, self.O)]
        peers += [self.dev(0, d, 0) for d in range(1, self.I)]
        peers += [self.dev(0, 0, d) for d in range(1, self.C)]
        for d in range(1, rows):
            peers.append((lax.rem(self.row + d, rows), lax.axis_index("cols")))
        for peer in peers:
            pl.semaphore_signal(sem, inc=1, device_id=peer, device_id_type=MESH)
        pl.semaphore_wait(sem, len(peers))


def gather_kernel(cols, root, branch, root_all, branch_all, zs, zr, ys, yr, cs, cr):
    at = Place(cols)
    O, I, C = at.O, at.I, at.C
    rb = root.shape[0]
    bb = branch.shape[1]

    def parts(i):
        return (
            root_all.at[pl.ds(pl.multiple_of(i * rb, rb), rb)],
            branch_all.at[:, pl.ds(pl.multiple_of(i * bb, bb), bb)],
        )

    sent = []

    def send(src, i, dev, ss, rs, slot):
        dst = parts(i)
        for k in range(2):
            cp = pltpu.make_async_remote_copy(
                src_ref=src[k], dst_ref=dst[k], send_sem=ss.at[slot, k], recv_sem=rs.at[slot, k],
                device_id=dev, device_id_type=MESH,
            )
            cp.start()
            sent.append(cp)

    def arrived(i, dev, ss, rs, slot):
        dst = parts(i)
        for k in range(2):
            pltpu.make_async_remote_copy(
                src_ref=dst[k], dst_ref=dst[k], send_sem=ss.at[slot, k], recv_sem=rs.at[slot, k],
                device_id=dev, device_id_type=MESH,
            ).wait_recv()

    at.greet()
    own = (root, branch)
    me = at.index(0, 0, 0)
    for dz in range(1, O):
        send(own, me, at.dev(dz, 0, 0), zs, zr, dz)
    for dy in range(1, I):
        send(own, me, at.dev(0, dy, 0), ys, yr, dy * O)
    for dc in range(1, C):
        send(own, me, at.dev(0, 0, dc), cs, cr, 0)
    mine = parts(me)
    mine[0][...] = root[...]
    mine[1][...] = branch[...]
    order = sorted(range(1, O), key=lambda d: min(d, O - d))
    for dz in order:
        i = at.index(-dz, 0, 0)
        arrived(i, at.dev(dz, 0, 0), zs, zr, dz)
        for dy in range(1, I):
            send(parts(i), i, at.dev(0, dy, 0), ys, yr, dy * O + dz)
        for dc in range(1, C):
            send(parts(i), i, at.dev(0, 0, dc), cs, cr, dz)
    for dz in [0] + order:
        for dy in range(1, I):
            i = at.index(-dz, -dy, 0)
            arrived(i, at.dev(0, dy, 0), ys, yr, dy * O + dz)
            for dc in range(1, C):
                send(parts(i), i, at.dev(0, 0, dc), cs, cr, dy * O + dz)
    for dc in range(1, C):
        for dy in range(I):
            for dz in [0] + order:
                arrived(at.index(-dz, -dy, -dc), at.dev(0, 0, dc), cs, cr, dy * O + dz)
    for cp in sent:
        cp.wait_send()


def gather(cols, root, branch):
    O, I, C = split_cols(cols)
    slots = O * I
    return pl.pallas_call(
        functools.partial(gather_kernel, cols),
        out_shape=(
            jax.ShapeDtypeStruct((root.shape[0] * cols, root.shape[1]), root.dtype),
            jax.ShapeDtypeStruct((branch.shape[0], branch.shape[1] * cols, branch.shape[2]), branch.dtype),
        ),
        in_specs=[VMEM] * 2,
        out_specs=(VMEM, VMEM),
        scratch_shapes=[pltpu.SemaphoreType.DMA((O, 2))] * 2 + [pltpu.SemaphoreType.DMA((slots, 2))] * 4,
        compiler_params=pltpu.CompilerParams(
            collective_id=0, has_side_effects=True, vmem_limit_bytes=16 << 20
        ),
        name="gather_kv",
    )(root, branch)


def reduce_kernel(
    rows, cols, root, branch, root_out, branch_out,
    rx1r, rx1b, s1, tx2, rx2, s2, tx3, rx3, rx4,
    a_s, a_r, b_s, b_r, c_s, c_r, d_s, d_r,
):
    at = Place(cols)
    O, I, C = at.O, at.I, at.C
    rb = root_out.shape[0]
    nb, bb, kw = branch_out.shape
    bf = nb * bb

    def parts(i):
        return (
            root.at[pl.ds(pl.multiple_of(i * rb, rb), rb)],
            branch.at[:, pl.ds(pl.multiple_of(i * bb, bb), bb)],
        )

    def copy(src, dst, ss, rs, dev):
        return pltpu.make_async_remote_copy(
            src_ref=src, dst_ref=dst, send_sem=ss, recv_sem=rs, device_id=dev, device_id_type=MESH
        )

    at.greet(rows)
    order = sorted(range(1, O), key=lambda d: -min(d, O - d)) + [0]
    pairs = [(dy, dz) for dy in list(range(1, I)) + [0] for dz in order]
    first = {}
    for dy, dz in pairs:
        slot = dy * O + dz
        for dc in range(1, C):
            src = parts(at.index(dz, dy, dc))
            dev = at.dev(0, 0, dc)
            first[dy, dz] = (
                copy(src[0], rx1r.at[slot], a_s.at[slot, 0], a_r.at[slot, 0], dev),
                copy(src[1], rx1b.at[slot], a_s.at[slot, 1], a_r.at[slot, 1], dev),
            )
            for cp in first[dy, dz]:
                cp.start()
    second = {}
    for dy, dz in pairs:
        slot = dy * O + dz
        own = parts(at.index(dz, dy, 0))
        r = own[0][...]
        b = own[1][...].reshape(bf, kw)
        if C > 1:
            for cp in first[dy, dz]:
                cp.wait_recv()
            r = r + rx1r[slot]
            b = b + rx1b[slot].reshape(bf, kw)
        if dy == 0:
            s1[dz, 0:rb] = r
            s1[dz, rb : rb + bf] = b
        else:
            tx2[slot - O, 0:rb] = r.astype(BF16)
            tx2[slot - O, rb : rb + bf] = b.astype(BF16)
            second[dy, dz] = copy(
                tx2.at[slot - O], rx2.at[slot - O], b_s.at[slot], b_r.at[slot], at.dev(0, dy, 0)
            )
            second[dy, dz].start()
    third = {}
    for dz in order:
        total = s1[dz]
        for dy in range(1, I):
            second[dy, dz].wait_recv()
            total = total + rx2[dy * O + dz - O].astype(F32)
        if dz == 0:
            s2[...] = total
        else:
            tx3[dz - 1] = total.astype(BF16)
            third[dz] = copy(
                tx3.at[dz - 1], rx3.at[dz - 1], c_s.at[dz], c_r.at[dz], at.dev(dz, 0, 0)
            )
            third[dz].start()
    total = s2[...]
    for dz in order[::-1][1:]:
        third[dz].wait_recv()
        total = total + rx3[dz - 1].astype(F32)
    branch_out[...] = total[rb : rb + bf].reshape(nb, bb, kw)
    rx4[at.row] = total[0:rb]
    fourth = []
    for dr in range(1, rows):
        dev = (lax.rem(at.row + dr, rows), lax.axis_index("cols"))
        cp = copy(rx4.at[at.row], rx4.at[at.row], d_s.at[dr], d_r.at[dr], dev)
        cp.start()
        fourth.append(cp)
    for dr in range(1, rows):
        row = lax.rem(at.row + rows - dr, rows)
        copy(rx4.at[row], rx4.at[row], d_s.at[dr], d_r.at[dr], (row, lax.axis_index("cols"))).wait_recv()
    out = rx4[0]
    for k in range(1, rows):
        out = out + rx4[k]
    root_out[...] = out
    for cps in first.values():
        for cp in cps:
            cp.wait_send()
    for cp in list(second.values()) + list(third.values()) + fourth:
        cp.wait_send()


def reduce(rows, cols, root, branch):
    O, I, C = split_cols(cols)
    slots = O * I
    rb = root.shape[0] // cols
    nb, blen, kw = branch.shape
    bb = blen // cols
    full = rb + nb * bb
    rest = max(slots - O, 1)
    dma = pltpu.SemaphoreType.DMA
    return pl.pallas_call(
        functools.partial(reduce_kernel, rows, cols),
        out_shape=(
            jax.ShapeDtypeStruct((rb, kw), F32),
            jax.ShapeDtypeStruct((nb, bb, kw), F32),
        ),
        in_specs=[VMEM] * 2,
        out_specs=(VMEM, VMEM),
        scratch_shapes=[
            pltpu.VMEM((slots, rb, kw), F32),
            pltpu.VMEM((slots, nb, bb, kw), F32),
            pltpu.VMEM((O, full, kw), F32),
            pltpu.VMEM((rest, full, kw), BF16),
            pltpu.VMEM((rest, full, kw), BF16),
            pltpu.VMEM((full, kw), F32),
            pltpu.VMEM((max(O - 1, 1), full, kw), BF16),
            pltpu.VMEM((max(O - 1, 1), full, kw), BF16),
            pltpu.VMEM((rows, rb, kw), F32),
            dma((slots, 2)), dma((slots, 2)), dma((slots,)), dma((slots,)),
            dma((O,)), dma((O,)), dma((rows,)), dma((rows,)),
        ],
        compiler_params=pltpu.CompilerParams(
            collective_id=1, has_side_effects=True, vmem_limit_bytes=32 << 20
        ),
        name="reduce_grads",
    )(root, branch)


def dot(a, b):
    return jnp.dot(a, b, preferred_element_type=F32)


def attend_kernel(
    lens_ref, segb_ref, q, o, g, ln_t, leaf, root, branch, seg,
    dq, leaf_g, root_g, branch_g,
    qt, gt, qs, gs, qt2, gt2, qs2, gs2, dqt, dst, pt, l2, delta,
):
    tok = q.shape[0]
    scale = HD ** (-0.5)
    nb = branch.shape[0]
    blen = branch.shape[1]
    row = lax.axis_index("rows")
    seg_row = seg[...]
    tb = jnp.zeros(seg_row.shape, jnp.int32)
    for s in range(segb_ref.shape[1]):
        tb = jnp.where(seg_row == s, segb_ref[0, s], tb)
    lens = [lens_ref[row * nb + b] for b in range(nb)]
    length = jnp.zeros(seg_row.shape, jnp.int32)
    for b in range(nb):
        length = jnp.where(tb == b, lens[b], length)
    tb_f = jnp.broadcast_to(tb.astype(F32), (HD, tok))
    tb_c = tb_f.T
    l2[...] = ln_t[...] * LOG2E
    for h in range(HEADS):
        hd = slice(h * HD, (h + 1) * HD)
        ht = slice(h * tok, (h + 1) * tok)
        qh = q[:, hd]
        gh = g[:, hd]
        qht = qh.T
        ght = gh.T
        delta[h : h + 1, :] = jnp.sum((gh.astype(F32) * o[:, hd].astype(F32)).T, axis=0, keepdims=True)
        qs[ht, :] = qh
        gs[ht, :] = gh
        qt[:, ht] = qht
        gt[:, ht] = ght
        for b in range(nb):
            bd = slice(b * HD, (b + 1) * HD)
            qs2[ht, bd] = jnp.where(tb_c == b, qh.astype(F32), 0.0).astype(BF16)
            gs2[ht, bd] = jnp.where(tb_c == b, gh.astype(F32), 0.0).astype(BF16)
            qt2[bd, ht] = jnp.where(tb_f == b, qht.astype(F32), 0.0).astype(BF16)
            gt2[bd, ht] = jnp.where(tb_f == b, ght.astype(F32), 0.0).astype(BF16)

    def block(k, v, qtr, gtr, qsr, gsr, allowed):
        for h in range(HEADS):
            ht = slice(h * tok, (h + 1) * tok)
            w = jnp.exp2(dot(k, qtr[:, ht]) * (scale * LOG2E) - l2[h : h + 1, :])
            if allowed is not None:
                w = jnp.where(allowed, w, 0.0)
            d = w * (dot(v, gtr[:, ht]) - delta[h : h + 1, :])
            pt[:, ht] = w.astype(BF16)
            dst[:, ht] = d.astype(BF16)
        ds = dst[...]
        return dot(ds, qsr[...]) * scale, dot(pt[...], gsr[...]), dot(k.T, ds)

    iota_k = lax.broadcasted_iota(jnp.int32, (tok, tok), 0)
    iota_t = lax.broadcasted_iota(jnp.int32, (tok, tok), 1)
    seg_b = jnp.broadcast_to(seg_row.astype(F32), (tok, tok))
    dk, dv, dqp = block(
        leaf[:, :HD], leaf[:, HD:], qt, gt, qs, gs, (seg_b == seg_b.T) & (iota_k <= iota_t)
    )
    leaf_g[:, :HD] = dk
    leaf_g[:, HD:] = dv
    dqt[...] = dqp

    longest = functools.reduce(jnp.maximum, lens)

    @pl.loop(0, blen // KB)
    def _(i):
        at = pl.ds(pl.multiple_of(i * KB, KB), KB)

        @pl.when(i * KB < longest)
        def _():
            pos = i * KB + lax.broadcasted_iota(jnp.int32, (KB, tok), 0)
            k = jnp.concatenate([branch[b, at, :HD] for b in range(nb)], axis=1)
            v = jnp.concatenate([branch[b, at, HD:] for b in range(nb)], axis=1)
            dk, dv, dqp = block(k, v, qt2, gt2, qs2, gs2, pos < length)
            for b in range(nb):
                bd = slice(b * HD, (b + 1) * HD)
                branch_g[b, at, :HD] = dk[:, bd]
                branch_g[b, at, HD:] = dv[:, bd]
            for h in range(HEADS):
                ht = slice(h * tok, (h + 1) * tok)
                part = dqp[:HD, ht]
                for b in range(1, nb):
                    part = jnp.where(tb_f == b, dqp[b * HD : (b + 1) * HD, ht], part)
                dqt[:, ht] += part

        @pl.when(i * KB >= longest)
        def _():
            for b in range(nb):
                branch_g[b, at, :] = jnp.zeros((KB, 2 * HD), F32)

    @pl.loop(0, root.shape[0] // KB)
    def _(i):
        at = pl.ds(pl.multiple_of(i * KB, KB), KB)
        dk, dv, dqp = block(root[at, :HD], root[at, HD:], qt, gt, qs, gs, None)
        root_g[at, :HD] = dk
        root_g[at, HD:] = dv
        dqt[...] += dqp

    for h in range(HEADS):
        dq[:, h * HD : (h + 1) * HD] = (dqt[:, h * tok : (h + 1) * tok].T * scale).astype(BF16)


def attend(lens, segb, q, o, g, ln_t, leaf, root, branch, seg):
    tok = q.shape[0]
    n = tok * HEADS
    nb = branch.shape[0]
    return pl.pallas_call(
        attend_kernel,
        out_shape=(
            jax.ShapeDtypeStruct(q.shape, BF16),
            jax.ShapeDtypeStruct(leaf.shape, F32),
            jax.ShapeDtypeStruct(root.shape, F32),
            jax.ShapeDtypeStruct(branch.shape, F32),
        ),
        in_specs=[SMEM] * 2 + [VMEM] * 8,
        out_specs=(VMEM,) * 4,
        scratch_shapes=[
            pltpu.VMEM((HD, n), BF16), pltpu.VMEM((HD, n), BF16),
            pltpu.VMEM((n, HD), BF16), pltpu.VMEM((n, HD), BF16),
            pltpu.VMEM((nb * HD, n), BF16), pltpu.VMEM((nb * HD, n), BF16),
            pltpu.VMEM((n, nb * HD), BF16), pltpu.VMEM((n, nb * HD), BF16),
            pltpu.VMEM((HD, n), F32),
            pltpu.VMEM((KB, n), BF16), pltpu.VMEM((KB, n), BF16),
            pltpu.VMEM((HEADS, tok), F32), pltpu.VMEM((HEADS, tok), F32),
        ],
        compiler_params=pltpu.CompilerParams(vmem_limit_bytes=48 << 20),
        name="attend_grads",
    )(lens, segb, q, o, g, ln_t, leaf, root, branch, seg)


def shards(rows, cols, q, o, g, log_norm, leaf, root, branch, lens, seg, segb):
    root_all, branch_all = gather(cols, root, branch)
    dq, leaf_g, root_g, branch_g = attend(
        lens, segb, q, o, g, log_norm.T, leaf, root_all, branch_all, seg
    )
    root_grad, branch_grad = reduce(rows, cols, root_g, branch_g)
    return dq, leaf_g, root_grad, branch_grad


def solution(mesh):
    both = P(("rows", "cols"), None)
    in_specs = (
        both, both, both, both, both, P("cols", None), P("rows", "cols", None), P(), both, both,
    )
    out_specs = (both, both, P("cols", None), P("rows", "cols", None))
    body = functools.partial(shards, mesh.shape["rows"], mesh.shape["cols"])
    return jax.shard_map(body, mesh=mesh, in_specs=in_specs, out_specs=out_specs, check_vma=False)
```

```python
import functools

import jax
import jax.numpy as jnp
from jax import lax
from jax.experimental import pallas as pl
from jax.experimental.pallas import tpu as pltpu
from jax.sharding import PartitionSpec as P

HEADS = 8
HD = 128
KB = 256
MESH = pl.DeviceIdType.MESH
F32 = jnp.float32
BF16 = jnp.bfloat16
LOG2E = 1.4426950408889634
VMEM = pl.BlockSpec(memory_space=pltpu.VMEM)
SMEM = pl.BlockSpec(memory_space=pltpu.SMEM)


def split_cols(cols):
    core = 2 if cols % 2 == 0 else 1
    chips = cols // core
    outer = 4 if chips % 4 == 0 else chips
    return outer, chips // outer, core


class Place:
    def __init__(self, cols):
        self.O, self.I, self.C = split_cols(cols)
        self.row = lax.axis_index("rows")
        me = lax.axis_index("cols")
        self.c = lax.rem(me, self.C)
        chip = me // self.C
        self.y = lax.rem(chip, self.I)
        self.z = chip // self.I

    def index(self, dz, dy, dc):
        z = lax.rem(self.z + dz + self.O, self.O)
        y = lax.rem(self.y + dy + self.I, self.I)
        c = lax.rem(self.c + dc + self.C, self.C)
        return (z * self.I + y) * self.C + c

    def dev(self, dz, dy, dc):
        return (self.row, self.index(dz, dy, dc))

    def greet(self, rows=1):
        sem = pltpu.get_barrier_semaphore()
        peers = [self.dev(d, 0, 0) for d in range(1, self.O)]
        peers += [self.dev(0, d, 0) for d in range(1, self.I)]
        peers += [self.dev(0, 0, d) for d in range(1, self.C)]
        for d in range(1, rows):
            peers.append((lax.rem(self.row + d, rows), lax.axis_index("cols")))
        for peer in peers:
            pl.semaphore_signal(sem, inc=1, device_id=peer, device_id_type=MESH)
        pl.semaphore_wait(sem, len(peers))


def dot(a, b):
    return jnp.dot(a, b, preferred_element_type=F32)


def fused_kernel(
    rows, cols,
    lens_ref, segb_ref, q_in, o_in, g_in, ln_t, leaf_in, root, branch, seg,
    dq, leaf_g, root_out, branch_out,
    q, o, g, leaf, root_all, branch_all, root_g, branch_g,
    qt, gt, qs, gs, qt2, gt2, qs2, gs2, dqt, dst, pt, l2, delta,
    rx1r, rx1b, s1r, s1b, tx2r, tx2b, rx2r, rx2b, tx3r, tx3b, rx3r, rx3b, rx4,
    loc, zs, zr, ys, yr, cs, cr, a_s, a_r, b_s, b_r, c_s, c_r, d_s, d_r,
):
    at = Place(cols)
    O, I, C = at.O, at.I, at.C
    rb = root.shape[0]
    nb, bb, _ = branch.shape
    blen = branch_all.shape[1]
    tok = q.shape[0]
    scale = HD ** (-0.5)
    kinds = (0, 1)
    rx1, s1 = (rx1r, rx1b), (s1r, s1b)
    tx2, rx2, tx3, rx3 = (tx2r, tx2b), (rx2r, rx2b), (tx3r, tx3b), (rx3r, rx3b)
    out = (root_out, branch_out)

    def part(pair, k, i):
        if k == 0:
            return pair[0].at[pl.ds(pl.multiple_of(i * rb, rb), rb)]
        return pair[1].at[:, pl.ds(pl.multiple_of(i * bb, bb), bb)]

    everything = (root_all, branch_all)
    grads = (root_g, branch_g)
    own = (root, branch)
    me = at.index(0, 0, 0)

    def copy(src, dst, ss, rs, dev):
        return pltpu.make_async_remote_copy(
            src_ref=src, dst_ref=dst, send_sem=ss, recv_sem=rs, device_id=dev, device_id_type=MESH
        )

    def z_copy(k, dz, i):
        src = part(everything, k, i)
        return copy(src, src, zs.at[dz, k], zr.at[dz, k], at.dev(dz, 0, 0))

    def y_copy(k, dy, dz, i):
        src = part(everything, k, i)
        slot = dy * O + dz
        return copy(src, src, ys.at[slot, k], yr.at[slot, k], at.dev(0, dy, 0))

    def c_copy(k, slot, i):
        src = part(everything, k, i)
        return copy(src, src, cs.at[slot, k], cr.at[slot, k], at.dev(0, 0, 1))

    def own_copies(k):
        dst = part(everything, k, me)
        made = [copy(own[k], dst, zs.at[d, k], zr.at[d, k], at.dev(d, 0, 0)) for d in range(1, O)]
        made += [
            copy(own[k], dst, ys.at[d * O, k], yr.at[d * O, k], at.dev(0, d, 0)) for d in range(1, I)
        ]
        if C > 1:
            made.append(copy(own[k], dst, cs.at[0, k], cr.at[0, k], at.dev(0, 0, 1)))
        return made

    def z_forward(k, dz):
        i = at.index(-dz, 0, 0)
        z_copy(k, dz, i).wait_recv()
        for dy in range(1, I):
            y_copy(k, dy, dz, i).start()
        if C > 1:
            c_copy(k, dz, i).start()

    def y_forward(k, dy, dz):
        i = at.index(-dz, -dy, 0)
        y_copy(k, dy, dz, i).wait_recv()
        if C > 1:
            c_copy(k, dy * O + dz, i).start()

    def c_arrive(k, dy, dz):
        if C > 1:
            c_copy(k, dy * O + dz, at.index(-dz, -dy, 1)).wait_recv()

    locals_ = [
        pltpu.make_async_copy(a, b, loc.at[n])
        for n, (a, b) in enumerate(
            [(q_in, q), (g_in, g), (o_in, o), (leaf_in, leaf)]
            + [(own[k], part(everything, k, me)) for k in kinds]
        )
    ]
    for cp in locals_:
        cp.start()
    at.greet(rows)
    sent = []
    for k in kinds:
        for cp in own_copies(k):
            cp.start()
            sent.append(cp)
    for cp in locals_:
        cp.wait()

    row = at.row
    seg_row = seg[...]
    tb = jnp.zeros(seg_row.shape, jnp.int32)
    for s in range(segb_ref.shape[1]):
        tb = jnp.where(seg_row == s, segb_ref[0, s], tb)
    length = jnp.zeros(seg_row.shape, jnp.int32)
    for b in range(nb):
        length = jnp.where(tb == b, lens_ref[row * nb + b], length)
    tb_f = jnp.broadcast_to(tb.astype(F32), (HD, tok))
    tb_c = tb_f.T
    l2[...] = ln_t[...] * LOG2E
    for h in range(HEADS):
        hd = slice(h * HD, (h + 1) * HD)
        ht = slice(h * tok, (h + 1) * tok)
        qh = q[:, hd]
        gh = g[:, hd]
        qht = qh.T
        ght = gh.T
        delta[h : h + 1, :] = jnp.sum((gh.astype(F32) * o[:, hd].astype(F32)).T, axis=0, keepdims=True)
        qs[ht, :] = qh
        gs[ht, :] = gh
        qt[:, ht] = qht
        gt[:, ht] = ght
        for b in range(nb):
            bd = slice(b * HD, (b + 1) * HD)
            qs2[ht, bd] = jnp.where(tb_c == b, qh.astype(F32), 0.0).astype(BF16)
            gs2[ht, bd] = jnp.where(tb_c == b, gh.astype(F32), 0.0).astype(BF16)
            qt2[bd, ht] = jnp.where(tb_f == b, qht.astype(F32), 0.0).astype(BF16)
            gt2[bd, ht] = jnp.where(tb_f == b, ght.astype(F32), 0.0).astype(BF16)

    def block(k, v, qtr, gtr, qsr, gsr, allowed):
        n = k.shape[0]
        for h in range(HEADS):
            ht = slice(h * tok, (h + 1) * tok)
            w = jnp.exp2(dot(k, qtr[:, ht]) * (scale * LOG2E) - l2[h : h + 1, :])
            if allowed is not None:
                w = jnp.where(allowed, w, 0.0)
            d = w * (dot(v, gtr[:, ht]) - delta[h : h + 1, :])
            pt[:n, ht] = w.astype(BF16)
            dst[:n, ht] = d.astype(BF16)
        ds = dst[:n]
        return dot(ds, qsr[...]) * scale, dot(pt[:n], gsr[...]), dot(k.T, ds)

    for dz in range(1, O):
        z_forward(0, dz)

    iota_k = lax.broadcasted_iota(jnp.int32, (tok, tok), 0)
    iota_t = lax.broadcasted_iota(jnp.int32, (tok, tok), 1)
    seg_b = jnp.broadcast_to(seg_row.astype(F32), (tok, tok))
    dk, dv, dqp = block(
        leaf[:, :HD], leaf[:, HD:], qt, gt, qs, gs, (seg_b == seg_b.T) & (iota_k <= iota_t)
    )
    leaf_g[:, :HD] = dk
    leaf_g[:, HD:] = dv
    dqt[...] = dqp

    for dy in range(1, I):
        for dz in range(O):
            y_forward(0, dy, dz)

    def mate_copy(k, chip):
        return copy(
            part(grads, k, chip * C + lax.rem(at.c + 1, C)), rx1[k].at[chip],
            a_s.at[chip, k], a_r.at[chip, k], at.dev(0, 0, 1),
        )

    rc = rb * C

    @pl.loop(0, O * I)
    def _(s):
        dz = lax.rem(s, O)
        dy = s // O

        @pl.when((dy == 0) & (dz > 0))
        def _():
            z_forward(1, dz)

        @pl.when(dy > 0)
        def _():
            i = at.index(-dz, -dy, 0)
            slot = dy * O + dz
            src = part(everything, 1, i)
            copy(src, src, ys.at[slot, 1], yr.at[slot, 1], at.dev(0, 0, 1)).wait_recv()
            if C > 1:
                c_copy(1, slot, i).start()

        c_arrive(0, dy, dz)
        chip = at.index(-dz, -dy, 0) // C
        keys = pl.ds(pl.multiple_of(chip * rc, rc), rc)
        dk, dv, dqp = block(root_all[keys, :HD], root_all[keys, HD:], qt, gt, qs, gs, None)
        root_g[keys, :HD] = dk
        root_g[keys, HD:] = dv
        dqt[...] += dqp
        if C > 1:
            mate_copy(0, chip).start()

    for dy in range(I):
        for dz in range(O):
            c_arrive(1, dy, dz)

    far = sorted(range(1, O), key=lambda d: -min(d, O - d)) + [0]
    pairs = [(dy, dz) for dy in list(range(1, I)) + [0] for dz in far]

    def second_copy(k, dy, dz):
        n = dy * O + dz - O
        return copy(
            tx2[k].at[n], rx2[k].at[n], b_s.at[n + O, k], b_r.at[n + O, k], at.dev(0, dy, 0)
        )

    def second(k):
        for dy, dz in pairs:
            i = at.index(dz, dy, 0)
            v = part(grads, k, i)[...]
            if C > 1:
                mate_copy(k, i // C).wait_recv()
                v = v + rx1[k][i // C]
            if dy == 0:
                s1[k][dz] = v
            else:
                tx2[k][dy * O + dz - O] = v.astype(BF16)
                second_copy(k, dy, dz).start()

    def third_copy(k, dz):
        return copy(
            tx3[k].at[dz - 1], rx3[k].at[dz - 1], c_s.at[dz, k], c_r.at[dz, k], at.dev(dz, 0, 0)
        )

    def third(k):
        for dz in far:
            total = s1[k][dz]
            for dy in range(1, I):
                second_copy(k, dy, dz).wait_recv()
                total = total + rx2[k][dy * O + dz - O].astype(F32)
            if dz == 0:
                s1[k][0] = total
            else:
                tx3[k][dz - 1] = total.astype(BF16)
                third_copy(k, dz).start()

    def last(k):
        total = s1[k][0]
        for dz in far[::-1][1:]:
            third_copy(k, dz).wait_recv()
            total = total + rx3[k][dz - 1].astype(F32)
        return total

    second(0)

    per = KB // (bb * C)

    @pl.loop(0, blen // KB)
    def _(i):
        keys = pl.ds(pl.multiple_of(i * KB, KB), KB)
        pos = i * KB + lax.broadcasted_iota(jnp.int32, (KB, tok), 0)
        k = jnp.concatenate([branch_all[b, keys, :HD] for b in range(nb)], axis=1)
        v = jnp.concatenate([branch_all[b, keys, HD:] for b in range(nb)], axis=1)
        dk, dv, dqp = block(k, v, qt2, gt2, qs2, gs2, pos < length)
        for b in range(nb):
            bd = slice(b * HD, (b + 1) * HD)
            branch_g[b, keys, :HD] = dk[:, bd]
            branch_g[b, keys, HD:] = dv[:, bd]
        for h in range(HEADS):
            ht = slice(h * tok, (h + 1) * tok)
            piece = dqp[:HD, ht]
            for b in range(1, nb):
                piece = jnp.where(tb_f == b, dqp[b * HD : (b + 1) * HD, ht], piece)
            dqt[:, ht] += piece
        if C > 1:
            for n in range(per):
                mate_copy(1, i * per + n).start()

    third(0)
    second(1)
    for h in range(HEADS):
        dq[:, h * HD : (h + 1) * HD] = (dqt[:, h * tok : (h + 1) * tok].T * scale).astype(BF16)

    rx4[row] = last(0)
    col = lax.axis_index("cols")

    def row_copy(dr, slot):
        dev = (lax.rem(row + dr, rows), col)
        return copy(rx4.at[slot], rx4.at[slot], d_s.at[dr], d_r.at[dr], dev)

    for dr in range(1, rows):
        row_copy(dr, row).start()
    third(1)
    for dr in range(1, rows):
        row_copy(dr, lax.rem(row + rows - dr, rows)).wait_recv()
    total = rx4[0]
    for n in range(1, rows):
        total = total + rx4[n]
    root_out[...] = total
    branch_out[...] = last(1)

    for cp in sent:
        cp.wait_send()
    for k in kinds:
        for dz in range(1, O):
            i = at.index(-dz, 0, 0)
            for dy in range(1, I):
                y_copy(k, dy, dz, i).wait_send()
            third_copy(k, dz).wait_send()
        for dy in range(I):
            for dz in range(O):
                if C > 1:
                    if dy + dz > 0:
                        c_copy(k, dy * O + dz, at.index(-dz, -dy, 0)).wait_send()
                    mate_copy(k, dy * O + dz).wait_send()
                if dy > 0:
                    second_copy(k, dy, dz).wait_send()
    for dr in range(1, rows):
        row_copy(dr, row).wait_send()


def shards(rows, cols, q, o, g, log_norm, leaf, root, branch, lens, seg, segb):
    O, I, C = split_cols(cols)
    slots = O * I
    tok = q.shape[0]
    n = tok * HEADS
    rb, kw = root.shape
    nb, bb, _ = branch.shape
    rest = max(slots - O, 1)
    rim = max(O - 1, 1)
    dma = pltpu.SemaphoreType.DMA
    V = pltpu.VMEM
    any_ = pl.BlockSpec(memory_space=pl.ANY)
    big = max(KB, tok, rb * C)

    def both(lead, dtype):
        return [V((lead, rb, kw), dtype), V((lead, nb, bb, kw), dtype)]

    return pl.pallas_call(
        functools.partial(fused_kernel, rows, cols),
        out_shape=(
            jax.ShapeDtypeStruct(q.shape, BF16),
            jax.ShapeDtypeStruct(leaf.shape, F32),
            jax.ShapeDtypeStruct(root.shape, F32),
            jax.ShapeDtypeStruct(branch.shape, F32),
        ),
        in_specs=[SMEM] * 2 + [any_] * 3 + [VMEM] + [any_] * 3 + [VMEM],
        out_specs=(VMEM,) * 4,
        scratch_shapes=[
            V(q.shape, BF16), V(q.shape, BF16), V(q.shape, BF16), V(leaf.shape, BF16),
            V((rb * cols, kw), BF16), V((nb, bb * cols, kw), BF16),
            V((rb * cols, kw), F32), V((nb, bb * cols, kw), F32),
            V((HD, n), BF16), V((HD, n), BF16), V((n, HD), BF16), V((n, HD), BF16),
            V((nb * HD, n), BF16), V((nb * HD, n), BF16),
            V((n, nb * HD), BF16), V((n, nb * HD), BF16),
            V((HD, n), F32), V((big, n), BF16), V((big, n), BF16),
            V((HEADS, tok), F32), V((HEADS, tok), F32),
            *both(slots, F32), *both(O, F32), *both(rest, BF16), *both(rest, BF16),
            *both(rim, BF16), *both(rim, BF16), V((rows, rb, kw), F32),
            dma((6,)), dma((O, 2)), dma((O, 2)),
            *[dma((slots, 2)) for _ in range(8)],
            dma((O, 2)), dma((O, 2)), dma((rows,)), dma((rows,)),
        ],
        compiler_params=pltpu.CompilerParams(
            collective_id=0, has_side_effects=True, vmem_limit_bytes=56 << 20
        ),
        name="fused_grads",
    )(lens, segb, q, o, g, log_norm.T, leaf, root, branch, seg)


def solution(mesh):
    both = P(("rows", "cols"), None)
    in_specs = (
        both, both, both, both, both, P("cols", None), P("rows", "cols", None), P(), both, both,
    )
    out_specs = (both, both, P("cols", None), P("rows", "cols", None))
    body = functools.partial(shards, mesh.shape["rows"], mesh.shape["cols"])
    return jax.shard_map(body, mesh=mesh, in_specs=in_specs, out_specs=out_specs, check_vma=False)
```

```python
import functools

import jax
import jax.numpy as jnp
from jax import lax
from jax.experimental import pallas as pl
from jax.experimental.pallas import tpu as pltpu
from jax.sharding import PartitionSpec as P

HEADS = 8
HD = 128
KB = 256
MESH = pl.DeviceIdType.MESH
F32 = jnp.float32
BF16 = jnp.bfloat16
LOG2E = 1.4426950408889634
VMEM = pl.BlockSpec(memory_space=pltpu.VMEM)
SMEM = pl.BlockSpec(memory_space=pltpu.SMEM)


def split_cols(cols):
    core = 2 if cols % 2 == 0 else 1
    chips = cols // core
    outer = 4 if chips % 4 == 0 else chips
    return outer, chips // outer, core


class Place:
    def __init__(self, cols):
        self.O, self.I, self.C = split_cols(cols)
        self.row = lax.axis_index("rows")
        me = lax.axis_index("cols")
        self.c = lax.rem(me, self.C)
        chip = me // self.C
        self.y = lax.rem(chip, self.I)
        self.z = chip // self.I

    def index(self, dz, dy, dc):
        z = lax.rem(self.z + dz + self.O, self.O)
        y = lax.rem(self.y + dy + self.I, self.I)
        c = lax.rem(self.c + dc + self.C, self.C)
        return (z * self.I + y) * self.C + c

    def dev(self, dz, dy, dc):
        return (self.row, self.index(dz, dy, dc))

    def greet(self, rows=1):
        sem = pltpu.get_barrier_semaphore()
        peers = [self.dev(d, 0, 0) for d in range(1, self.O)]
        peers += [self.dev(0, d, 0) for d in range(1, self.I)]
        peers += [self.dev(0, 0, d) for d in range(1, self.C)]
        for d in range(1, rows):
            peers.append((lax.rem(self.row + d, rows), lax.axis_index("cols")))
        for peer in peers:
            pl.semaphore_signal(sem, inc=1, device_id=peer, device_id_type=MESH)
        pl.semaphore_wait(sem, len(peers))


def dot(a, b):
    return jnp.dot(a, b, preferred_element_type=F32)


def fused_kernel(
    rows, cols,
    lens_ref, segb_ref, q_in, o_in, g_in, ln_t, leaf_in, root, branch, seg,
    dq, leaf_g, root_out, branch_out,
    q, o, g, leaf, root_all, branch_all, root_g, branch_g,
    qt, gt, qs, gs, qt2, gt2, qs2, gs2, dqt, dst, pt, l2, delta,
    rx1r, rx1b, s1r, s1b, tx2r, tx2b, rx2r, rx2b, tx3r, tx3b, rx3r, rx3b, rx4,
    loc, zs, zr, ys, yr, cs, cr, a_s, a_r, b_s, b_r, c_s, c_r, d_s, d_r,
):
    at = Place(cols)
    O, I, C = at.O, at.I, at.C
    rb = root.shape[0]
    nb, bb, _ = branch.shape
    blen = branch_all.shape[1]
    tok = q.shape[0]
    scale = HD ** (-0.5)
    kinds = (0, 1)
    rx1, s1 = (rx1r, rx1b), (s1r, s1b)
    tx2, rx2, tx3, rx3 = (tx2r, tx2b), (rx2r, rx2b), (tx3r, tx3b), (rx3r, rx3b)
    out = (root_out, branch_out)

    def part(pair, k, i):
        if k == 0:
            return pair[0].at[pl.ds(pl.multiple_of(i * rb, rb), rb)]
        return pair[1].at[:, pl.ds(pl.multiple_of(i * bb, bb), bb)]

    everything = (root_all, branch_all)
    grads = (root_g, branch_g)
    own = (root, branch)
    me = at.index(0, 0, 0)

    def copy(src, dst, ss, rs, dev):
        return pltpu.make_async_remote_copy(
            src_ref=src, dst_ref=dst, send_sem=ss, recv_sem=rs, device_id=dev, device_id_type=MESH
        )

    def z_copy(k, dz, i):
        src = part(everything, k, i)
        return copy(src, src, zs.at[dz, k], zr.at[dz, k], at.dev(dz, 0, 0))

    def y_copy(k, dy, dz, i):
        src = part(everything, k, i)
        slot = dy * O + dz
        return copy(src, src, ys.at[slot, k], yr.at[slot, k], at.dev(0, dy, 0))

    def c_copy(k, slot, i):
        src = part(everything, k, i)
        return copy(src, src, cs.at[slot, k], cr.at[slot, k], at.dev(0, 0, 1))

    def own_copies(k):
        dst = part(everything, k, me)
        made = [copy(own[k], dst, zs.at[d, k], zr.at[d, k], at.dev(d, 0, 0)) for d in range(1, O)]
        made += [
            copy(own[k], dst, ys.at[d * O, k], yr.at[d * O, k], at.dev(0, d, 0)) for d in range(1, I)
        ]
        if C > 1:
            made.append(copy(own[k], dst, cs.at[0, k], cr.at[0, k], at.dev(0, 0, 1)))
        return made

    def z_forward(k, dz):
        i = at.index(-dz, 0, 0)
        z_copy(k, dz, i).wait_recv()
        for dy in range(1, I):
            y_copy(k, dy, dz, i).start()
        if C > 1:
            c_copy(k, dz, i).start()

    def y_forward(k, dy, dz):
        i = at.index(-dz, -dy, 0)
        y_copy(k, dy, dz, i).wait_recv()
        if C > 1:
            c_copy(k, dy * O + dz, i).start()

    def c_arrive(k, dy, dz):
        if C > 1:
            c_copy(k, dy * O + dz, at.index(-dz, -dy, 1)).wait_recv()

    locals_ = [
        pltpu.make_async_copy(a, b, loc.at[n])
        for n, (a, b) in enumerate(
            [(q_in, q), (g_in, g), (o_in, o), (leaf_in, leaf)]
            + [(own[k], part(everything, k, me)) for k in kinds]
        )
    ]
    for cp in locals_:
        cp.start()
    at.greet(rows)
    sent = []
    for cp in own_copies(0):
        cp.start()
        sent.append(cp)
    for cp in locals_:
        cp.wait()

    row = at.row
    seg_row = seg[...]
    tb = jnp.zeros(seg_row.shape, jnp.int32)
    for s in range(segb_ref.shape[1]):
        tb = jnp.where(seg_row == s, segb_ref[0, s], tb)
    length = jnp.zeros(seg_row.shape, jnp.int32)
    for b in range(nb):
        length = jnp.where(tb == b, lens_ref[row * nb + b], length)
    tb_f = jnp.broadcast_to(tb.astype(F32), (HD, tok))
    tb_c = tb_f.T
    l2[...] = ln_t[...] * LOG2E
    for h in range(HEADS):
        hd = slice(h * HD, (h + 1) * HD)
        ht = slice(h * tok, (h + 1) * tok)
        qh = q[:, hd]
        gh = g[:, hd]
        qht = qh.T
        ght = gh.T
        delta[h : h + 1, :] = jnp.sum((gh.astype(F32) * o[:, hd].astype(F32)).T, axis=0, keepdims=True)
        qs[ht, :] = qh
        gs[ht, :] = gh
        qt[:, ht] = qht
        gt[:, ht] = ght
        for b in range(nb):
            bd = slice(b * HD, (b + 1) * HD)
            qs2[ht, bd] = jnp.where(tb_c == b, qh.astype(F32), 0.0).astype(BF16)
            gs2[ht, bd] = jnp.where(tb_c == b, gh.astype(F32), 0.0).astype(BF16)
            qt2[bd, ht] = jnp.where(tb_f == b, qht.astype(F32), 0.0).astype(BF16)
            gt2[bd, ht] = jnp.where(tb_f == b, ght.astype(F32), 0.0).astype(BF16)

    def block(k, v, qtr, gtr, qsr, gsr, allowed):
        n = k.shape[0]
        for h in range(HEADS):
            ht = slice(h * tok, (h + 1) * tok)
            w = jnp.exp2(dot(k, qtr[:, ht]) * (scale * LOG2E) - l2[h : h + 1, :])
            if allowed is not None:
                w = jnp.where(allowed, w, 0.0)
            d = w * (dot(v, gtr[:, ht]) - delta[h : h + 1, :])
            pt[:n, ht] = w.astype(BF16)
            dst[:n, ht] = d.astype(BF16)
        ds = dst[:n]
        return dot(ds, qsr[...]) * scale, dot(pt[:n], gsr[...]), dot(k.T, ds)

    for dz in range(1, O):
        z_forward(0, dz)
    for cp in own_copies(1):
        cp.start()
        sent.append(cp)

    iota_k = lax.broadcasted_iota(jnp.int32, (tok, tok), 0)
    iota_t = lax.broadcasted_iota(jnp.int32, (tok, tok), 1)
    seg_b = jnp.broadcast_to(seg_row.astype(F32), (tok, tok))
    dk, dv, dqp = block(
        leaf[:, :HD], leaf[:, HD:], qt, gt, qs, gs, (seg_b == seg_b.T) & (iota_k <= iota_t)
    )
    leaf_g[:, :HD] = dk
    leaf_g[:, HD:] = dv
    dqt[...] = dqp

    def mate_copy(k, chip):
        return copy(
            part(grads, k, chip * C + lax.rem(at.c + 1, C)), rx1[k].at[chip],
            a_s.at[chip, k], a_r.at[chip, k], at.dev(0, 0, 1),
        )

    rc = rb * C

    def second_copy(k, dy, dz):
        n = dy * O + dz - O
        return copy(
            tx2[k].at[n], rx2[k].at[n], b_s.at[n + O, k], b_r.at[n + O, k], at.dev(0, dy, 0)
        )

    def second(k, chip):
        dz = lax.rem(chip // I - at.z + O, O)
        dy = lax.rem(lax.rem(chip, I) - at.y + I, I)
        v = part(grads, k, chip * C + at.c)[...]
        if C > 1:
            mate_copy(k, chip).wait_recv()
            v = v + rx1[k][chip]

        @pl.when(dy == 0)
        def _():
            s1[k][dz] = v

        if I > 1:

            @pl.when(dy > 0)
            def _():
                tx2[k][dy * O + dz - O] = v.astype(BF16)
                second_copy(k, dy, dz).start()

    @pl.loop(0, O * I)
    def _(s):
        dz = lax.rem(s, O)
        dy = s // O

        if I > 1:

            @pl.when(dy < I - 1)
            def _():
                y_forward(0, dy + 1, dz)

        @pl.when((dy == 0) & (dz > 0))
        def _():
            z_forward(1, dz)

        if I > 1:

            @pl.when(dy > 0)
            def _():
                y_forward(1, dy, dz)

        c_arrive(0, dy, dz)
        chip = at.index(-dz, -dy, 0) // C
        keys = pl.ds(pl.multiple_of(chip * rc, rc), rc)
        dk, dv, dqp = block(root_all[keys, :HD], root_all[keys, HD:], qt, gt, qs, gs, None)
        root_g[keys, :HD] = dk
        root_g[keys, HD:] = dv
        dqt[...] += dqp
        if C > 1:
            mate_copy(0, chip).start()

        @pl.when(s > 0)
        def _():
            p = s - 1
            second(0, at.index(-lax.rem(p, O), -(p // O), 0) // C)

    for dy in range(I):
        for dz in range(O):
            c_arrive(1, dy, dz)

    far = sorted(range(1, O), key=lambda d: -min(d, O - d)) + [0]

    def third_copy(k, dz):
        return copy(
            tx3[k].at[dz - 1], rx3[k].at[dz - 1], c_s.at[dz, k], c_r.at[dz, k], at.dev(dz, 0, 0)
        )

    def third(k):
        for dz in far:
            total = s1[k][dz]
            for dy in range(1, I):
                second_copy(k, dy, dz).wait_recv()
                total = total + rx2[k][dy * O + dz - O].astype(F32)
            if dz == 0:
                s1[k][0] = total
            else:
                tx3[k][dz - 1] = total.astype(BF16)
                third_copy(k, dz).start()

    def last(k):
        total = s1[k][0]
        for dz in far[::-1][1:]:
            third_copy(k, dz).wait_recv()
            total = total + rx3[k][dz - 1].astype(F32)
        return total

    second(0, at.index(-(O - 1), -(I - 1), 0) // C)

    per = KB // (bb * C)
    steps = blen // KB

    @pl.loop(0, steps)
    def _(i):
        keys = pl.ds(pl.multiple_of(i * KB, KB), KB)
        pos = i * KB + lax.broadcasted_iota(jnp.int32, (KB, tok), 0)
        k = jnp.concatenate([branch_all[b, keys, :HD] for b in range(nb)], axis=1)
        v = jnp.concatenate([branch_all[b, keys, HD:] for b in range(nb)], axis=1)
        dk, dv, dqp = block(k, v, qt2, gt2, qs2, gs2, pos < length)
        for b in range(nb):
            bd = slice(b * HD, (b + 1) * HD)
            branch_g[b, keys, :HD] = dk[:, bd]
            branch_g[b, keys, HD:] = dv[:, bd]
        for h in range(HEADS):
            ht = slice(h * tok, (h + 1) * tok)
            piece = dqp[:HD, ht]
            for b in range(1, nb):
                piece = jnp.where(tb_f == b, dqp[b * HD : (b + 1) * HD, ht], piece)
            dqt[:, ht] += piece
        if C > 1:
            for n in range(per):
                mate_copy(1, i * per + n).start()

        @pl.when(i > 0)
        def _():
            for n in range(per):
                second(1, (i - 1) * per + n)

        @pl.when(i == min(2, steps - 1))
        def _():
            third(0)

    for n in range(per):
        second(1, (steps - 1) * per + n)
    third(1)
    for h in range(HEADS):
        dq[:, h * HD : (h + 1) * HD] = (dqt[:, h * tok : (h + 1) * tok].T * scale).astype(BF16)

    rx4[row] = last(0)
    col = lax.axis_index("cols")

    def row_copy(dr, slot):
        dev = (lax.rem(row + dr, rows), col)
        return copy(rx4.at[slot], rx4.at[slot], d_s.at[dr], d_r.at[dr], dev)

    for dr in range(1, rows):
        row_copy(dr, row).start()
    for dr in range(1, rows):
        row_copy(dr, lax.rem(row + rows - dr, rows)).wait_recv()
    total = rx4[0]
    for n in range(1, rows):
        total = total + rx4[n]
    root_out[...] = total
    branch_out[...] = last(1)

    for cp in sent:
        cp.wait_send()
    for k in kinds:
        for dz in range(1, O):
            i = at.index(-dz, 0, 0)
            for dy in range(1, I):
                y_copy(k, dy, dz, i).wait_send()
            third_copy(k, dz).wait_send()
        for dy in range(I):
            for dz in range(O):
                if C > 1:
                    if dy + dz > 0:
                        c_copy(k, dy * O + dz, at.index(-dz, -dy, 0)).wait_send()
                    mate_copy(k, dy * O + dz).wait_send()
                if dy > 0:
                    second_copy(k, dy, dz).wait_send()
    for dr in range(1, rows):
        row_copy(dr, row).wait_send()


def shards(rows, cols, q, o, g, log_norm, leaf, root, branch, lens, seg, segb):
    O, I, C = split_cols(cols)
    slots = O * I
    tok = q.shape[0]
    n = tok * HEADS
    rb, kw = root.shape
    nb, bb, _ = branch.shape
    rest = max(slots - O, 1)
    rim = max(O - 1, 1)
    dma = pltpu.SemaphoreType.DMA
    V = pltpu.VMEM
    any_ = pl.BlockSpec(memory_space=pl.ANY)
    big = max(KB, tok, rb * C)

    def both(lead, dtype):
        return [V((lead, rb, kw), dtype), V((lead, nb, bb, kw), dtype)]

    return pl.pallas_call(
        functools.partial(fused_kernel, rows, cols),
        out_shape=(
            jax.ShapeDtypeStruct(q.shape, BF16),
            jax.ShapeDtypeStruct(leaf.shape, F32),
            jax.ShapeDtypeStruct(root.shape, F32),
            jax.ShapeDtypeStruct(branch.shape, F32),
        ),
        in_specs=[SMEM] * 2 + [any_] * 3 + [VMEM] + [any_] * 3 + [VMEM],
        out_specs=(VMEM,) * 4,
        scratch_shapes=[
            V(q.shape, BF16), V(q.shape, BF16), V(q.shape, BF16), V(leaf.shape, BF16),
            V((rb * cols, kw), BF16), V((nb, bb * cols, kw), BF16),
            V((rb * cols, kw), F32), V((nb, bb * cols, kw), F32),
            V((HD, n), BF16), V((HD, n), BF16), V((n, HD), BF16), V((n, HD), BF16),
            V((nb * HD, n), BF16), V((nb * HD, n), BF16),
            V((n, nb * HD), BF16), V((n, nb * HD), BF16),
            V((HD, n), F32), V((big, n), BF16), V((big, n), BF16),
            V((HEADS, tok), F32), V((HEADS, tok), F32),
            *both(slots, F32), *both(O, F32), *both(rest, BF16), *both(rest, BF16),
            *both(rim, BF16), *both(rim, BF16), V((rows, rb, kw), F32),
            dma((6,)), dma((O, 2)), dma((O, 2)),
            *[dma((slots, 2)) for _ in range(8)],
            dma((O, 2)), dma((O, 2)), dma((rows,)), dma((rows,)),
        ],
        compiler_params=pltpu.CompilerParams(
            collective_id=0, has_side_effects=True, vmem_limit_bytes=56 << 20
        ),
        name="fused_grads",
    )(lens, segb, q, o, g, log_norm.T, leaf, root, branch, seg)


def solution(mesh):
    both = P(("rows", "cols"), None)
    in_specs = (
        both, both, both, both, both, P("cols", None), P("rows", "cols", None), P(), both, both,
    )
    out_specs = (both, both, P("cols", None), P("rows", "cols", None))
    body = functools.partial(shards, mesh.shape["rows"], mesh.shape["cols"])
    return jax.shard_map(body, mesh=mesh, in_specs=in_specs, out_specs=out_specs, check_vma=False)
```

```python
import functools

import jax
import jax.numpy as jnp
from jax import lax
from jax.experimental import pallas as pl
from jax.experimental.pallas import tpu as pltpu
from jax.sharding import PartitionSpec as P

HEADS = 8
HD = 128
KB = 256
MESH = pl.DeviceIdType.MESH
F32 = jnp.float32
BF16 = jnp.bfloat16
LOG2E = 1.4426950408889634
VMEM = pl.BlockSpec(memory_space=pltpu.VMEM)
SMEM = pl.BlockSpec(memory_space=pltpu.SMEM)


def split_cols(cols):
    core = 2 if cols % 2 == 0 else 1
    chips = cols // core
    outer = 4 if chips % 4 == 0 else chips
    return outer, chips // outer, core


class Place:
    def __init__(self, cols):
        self.O, self.I, self.C = split_cols(cols)
        self.row = lax.axis_index("rows")
        me = lax.axis_index("cols")
        self.c = lax.rem(me, self.C)
        chip = me // self.C
        self.y = lax.rem(chip, self.I)
        self.z = chip // self.I

    def index(self, dz, dy, dc):
        z = lax.rem(self.z + dz + self.O, self.O)
        y = lax.rem(self.y + dy + self.I, self.I)
        c = lax.rem(self.c + dc + self.C, self.C)
        return (z * self.I + y) * self.C + c

    def dev(self, dz, dy, dc):
        return (self.row, self.index(dz, dy, dc))

    def greet(self, rows=1):
        sem = pltpu.get_barrier_semaphore()
        peers = [self.dev(d, 0, 0) for d in range(1, self.O)]
        peers += [self.dev(0, d, 0) for d in range(1, self.I)]
        peers += [self.dev(0, 0, d) for d in range(1, self.C)]
        for d in range(1, rows):
            peers.append((lax.rem(self.row + d, rows), lax.axis_index("cols")))
        for peer in peers:
            pl.semaphore_signal(sem, inc=1, device_id=peer, device_id_type=MESH)
        pl.semaphore_wait(sem, len(peers))


def dot(a, b):
    return jnp.dot(a, b, preferred_element_type=F32)


def fused_kernel(
    rows, cols,
    lens_ref, segb_ref, q_in, o_in, g_in, ln_t, leaf_in, root, branch, seg,
    dq, leaf_g, root_out, branch_out,
    q, o, g, leaf, root_all, branch_all, root_g, branch_g,
    qt, gt, qs, gs, qt2, gt2, qs2, gs2, dqt, dst, pt, l2, delta,
    rx1r, rx1b, s1r, s1b, tx2r, tx2b, rx2r, rx2b, tx3r, tx3b, rx3r, rx3b, rx4,
    loc, zs, zr, ys, yr, cs, cr, a_s, a_r, b_s, b_r, c_s, c_r, d_s, d_r,
):
    at = Place(cols)
    O, I, C = at.O, at.I, at.C
    rb = root.shape[0]
    nb, bb, _ = branch.shape
    blen = branch_all.shape[1]
    tok = q.shape[0]
    scale = HD ** (-0.5)
    kinds = (0, 1)
    rx1, s1 = (rx1r, rx1b), (s1r, s1b)
    tx2, rx2, tx3, rx3 = (tx2r, tx2b), (rx2r, rx2b), (tx3r, tx3b), (rx3r, rx3b)
    out = (root_out, branch_out)

    def part(pair, k, i):
        if k == 0:
            return pair[0].at[pl.ds(pl.multiple_of(i * rb, rb), rb)]
        return pair[1].at[:, pl.ds(pl.multiple_of(i * bb, bb), bb)]

    everything = (root_all, branch_all)
    grads = (root_g, branch_g)
    own = (root, branch)
    me = at.index(0, 0, 0)

    def copy(src, dst, ss, rs, dev):
        return pltpu.make_async_remote_copy(
            src_ref=src, dst_ref=dst, send_sem=ss, recv_sem=rs, device_id=dev, device_id_type=MESH
        )

    def z_copy(k, dz, i):
        src = part(everything, k, i)
        return copy(src, src, zs.at[dz, k], zr.at[dz, k], at.dev(dz, 0, 0))

    def y_copy(k, dy, dz, i):
        src = part(everything, k, i)
        slot = dy * O + dz
        return copy(src, src, ys.at[slot, k], yr.at[slot, k], at.dev(0, dy, 0))

    def c_copy(k, slot, i):
        src = part(everything, k, i)
        return copy(src, src, cs.at[slot, k], cr.at[slot, k], at.dev(0, 0, 1))

    def own_copies(k):
        dst = part(everything, k, me)
        made = [copy(own[k], dst, zs.at[d, k], zr.at[d, k], at.dev(d, 0, 0)) for d in range(1, O)]
        made += [
            copy(own[k], dst, ys.at[d * O, k], yr.at[d * O, k], at.dev(0, d, 0)) for d in range(1, I)
        ]
        if C > 1:
            made.append(copy(own[k], dst, cs.at[0, k], cr.at[0, k], at.dev(0, 0, 1)))
        return made

    def z_forward(k, dz):
        i = at.index(-dz, 0, 0)
        z_copy(k, dz, i).wait_recv()
        for dy in range(1, I):
            y_copy(k, dy, dz, i).start()
        if C > 1:
            c_copy(k, dz, i).start()

    def y_forward(k, dy, dz):
        i = at.index(-dz, -dy, 0)
        y_copy(k, dy, dz, i).wait_recv()
        if C > 1:
            c_copy(k, dy * O + dz, i).start()

    def c_arrive(k, dy, dz):
        if C > 1:
            c_copy(k, dy * O + dz, at.index(-dz, -dy, 1)).wait_recv()

    locals_ = [
        pltpu.make_async_copy(a, b, loc.at[n])
        for n, (a, b) in enumerate(
            [(q_in, q), (g_in, g), (o_in, o), (leaf_in, leaf)]
            + [(own[k], part(everything, k, me)) for k in kinds]
        )
    ]
    for cp in locals_:
        cp.start()
    at.greet(rows)
    sent = []
    for cp in own_copies(0):
        cp.start()
        sent.append(cp)
    for cp in locals_:
        cp.wait()

    row = at.row
    seg_row = seg[...]
    tb = jnp.zeros(seg_row.shape, jnp.int32)
    for s in range(segb_ref.shape[1]):
        tb = jnp.where(seg_row == s, segb_ref[0, s], tb)
    length = jnp.zeros(seg_row.shape, jnp.int32)
    for b in range(nb):
        length = jnp.where(tb == b, lens_ref[row * nb + b], length)
    tb_f = jnp.broadcast_to(tb.astype(F32), (HD, tok))
    tb_c = tb_f.T
    l2[...] = ln_t[...] * LOG2E
    for h in range(HEADS):
        hd = slice(h * HD, (h + 1) * HD)
        ht = slice(h * tok, (h + 1) * tok)
        qh = q[:, hd]
        gh = g[:, hd]
        qht = qh.T
        ght = gh.T
        delta[h : h + 1, :] = jnp.sum((gh.astype(F32) * o[:, hd].astype(F32)).T, axis=0, keepdims=True)
        qs[ht, :] = qh
        gs[ht, :] = gh
        qt[:, ht] = qht
        gt[:, ht] = ght
        for b in range(nb):
            bd = slice(b * HD, (b + 1) * HD)
            qs2[ht, bd] = jnp.where(tb_c == b, qh.astype(F32), 0.0).astype(BF16)
            gs2[ht, bd] = jnp.where(tb_c == b, gh.astype(F32), 0.0).astype(BF16)
            qt2[bd, ht] = jnp.where(tb_f == b, qht.astype(F32), 0.0).astype(BF16)
            gt2[bd, ht] = jnp.where(tb_f == b, ght.astype(F32), 0.0).astype(BF16)

    def block(k, v, qtr, gtr, qsr, gsr, allowed):
        n = k.shape[0]
        for h in range(HEADS):
            ht = slice(h * tok, (h + 1) * tok)
            w = jnp.exp2(dot(k, qtr[:, ht]) * (scale * LOG2E) - l2[h : h + 1, :])
            if allowed is not None:
                w = jnp.where(allowed, w, 0.0)
            d = w * (dot(v, gtr[:, ht]) - delta[h : h + 1, :])
            pt[:n, ht] = w.astype(BF16)
            dst[:n, ht] = d.astype(BF16)
        ds = dst[:n]
        return dot(ds, qsr[...]) * scale, dot(pt[:n], gsr[...]), dot(k.T, ds)

    for dz in range(1, O):
        z_forward(0, dz)
    for cp in own_copies(1):
        cp.start()
        sent.append(cp)

    iota_k = lax.broadcasted_iota(jnp.int32, (tok, tok), 0)
    iota_t = lax.broadcasted_iota(jnp.int32, (tok, tok), 1)
    seg_b = jnp.broadcast_to(seg_row.astype(F32), (tok, tok))
    dk, dv, dqp = block(
        leaf[:, :HD], leaf[:, HD:], qt, gt, qs, gs, (seg_b == seg_b.T) & (iota_k <= iota_t)
    )
    leaf_g[:, :HD] = dk
    leaf_g[:, HD:] = dv
    dqt[...] = dqp

    def mate_copy(k, chip):
        return copy(
            part(grads, k, chip * C + lax.rem(at.c + 1, C)), rx1[k].at[chip],
            a_s.at[chip, k], a_r.at[chip, k], at.dev(0, 0, 1),
        )

    rc = rb * C

    def second_copy(k, dy, dz):
        n = dy * O + dz - O
        return copy(
            tx2[k].at[n], rx2[k].at[n], b_s.at[n + O, k], b_r.at[n + O, k], at.dev(0, dy, 0)
        )

    def second(k, chip):
        dz = lax.rem(chip // I - at.z + O, O)
        dy = lax.rem(lax.rem(chip, I) - at.y + I, I)
        v = part(grads, k, chip * C + at.c)[...]
        if C > 1:
            mate_copy(k, chip).wait_recv()
            v = v + rx1[k][chip]

        @pl.when(dy == 0)
        def _():
            s1[k][dz] = v

        if I > 1:

            @pl.when(dy > 0)
            def _():
                tx2[k][dy * O + dz - O] = v.astype(BF16)
                second_copy(k, dy, dz).start()

    @pl.loop(0, O * I)
    def _(s):
        dz = lax.rem(s, O)
        dy = s // O

        if I > 1:

            @pl.when(dy < I - 1)
            def _():
                y_forward(0, dy + 1, dz)

        if I > 1:

            @pl.when(dy > 0)
            def _():
                y_forward(1, dy, dz)

        c_arrive(0, dy, dz)
        chip = at.index(-dz, -dy, 0) // C
        keys = pl.ds(pl.multiple_of(chip * rc, rc), rc)
        dk, dv, dqp = block(root_all[keys, :HD], root_all[keys, HD:], qt, gt, qs, gs, None)
        root_g[keys, :HD] = dk
        root_g[keys, HD:] = dv
        dqt[...] += dqp
        if C > 1:
            mate_copy(0, chip).start()

        @pl.when((dy == 0) & (dz > 0))
        def _():
            z_forward(1, dz)

        @pl.when(s > 0)
        def _():
            p = s - 1
            second(0, at.index(-lax.rem(p, O), -(p // O), 0) // C)

    for dy in range(I):
        for dz in range(O):
            c_arrive(1, dy, dz)

    far = sorted(range(1, O), key=lambda d: -min(d, O - d)) + [0]

    def third_copy(k, dz):
        return copy(
            tx3[k].at[dz - 1], rx3[k].at[dz - 1], c_s.at[dz, k], c_r.at[dz, k], at.dev(dz, 0, 0)
        )

    def third(k):
        for dz in far:
            total = s1[k][dz]
            for dy in range(1, I):
                second_copy(k, dy, dz).wait_recv()
                total = total + rx2[k][dy * O + dz - O].astype(F32)
            if dz == 0:
                s1[k][0] = total
            else:
                tx3[k][dz - 1] = total.astype(BF16)
                third_copy(k, dz).start()

    def last(k):
        total = s1[k][0]
        for dz in far[::-1][1:]:
            third_copy(k, dz).wait_recv()
            total = total + rx3[k][dz - 1].astype(F32)
        return total

    second(0, at.index(-(O - 1), -(I - 1), 0) // C)

    per = KB // (bb * C)
    steps = blen // KB

    @pl.loop(0, steps)
    def _(i):
        keys = pl.ds(pl.multiple_of(i * KB, KB), KB)
        pos = i * KB + lax.broadcasted_iota(jnp.int32, (KB, tok), 0)
        k = jnp.concatenate([branch_all[b, keys, :HD] for b in range(nb)], axis=1)
        v = jnp.concatenate([branch_all[b, keys, HD:] for b in range(nb)], axis=1)
        dk, dv, dqp = block(k, v, qt2, gt2, qs2, gs2, pos < length)
        for b in range(nb):
            bd = slice(b * HD, (b + 1) * HD)
            branch_g[b, keys, :HD] = dk[:, bd]
            branch_g[b, keys, HD:] = dv[:, bd]
        for h in range(HEADS):
            ht = slice(h * tok, (h + 1) * tok)
            piece = dqp[:HD, ht]
            for b in range(1, nb):
                piece = jnp.where(tb_f == b, dqp[b * HD : (b + 1) * HD, ht], piece)
            dqt[:, ht] += piece
        if C > 1:
            for n in range(per):
                mate_copy(1, i * per + n).start()

        @pl.when(i > 0)
        def _():
            for n in range(per):
                second(1, (i - 1) * per + n)

        @pl.when(i == min(2, steps - 1))
        def _():
            third(0)

    for n in range(per):
        second(1, (steps - 1) * per + n)
    third(1)
    for h in range(HEADS):
        dq[:, h * HD : (h + 1) * HD] = (dqt[:, h * tok : (h + 1) * tok].T * scale).astype(BF16)

    rx4[row] = last(0)
    col = lax.axis_index("cols")

    def row_copy(dr, slot):
        dev = (lax.rem(row + dr, rows), col)
        return copy(rx4.at[slot], rx4.at[slot], d_s.at[dr], d_r.at[dr], dev)

    for dr in range(1, rows):
        row_copy(dr, row).start()
    for dr in range(1, rows):
        row_copy(dr, lax.rem(row + rows - dr, rows)).wait_recv()
    total = rx4[0]
    for n in range(1, rows):
        total = total + rx4[n]
    root_out[...] = total
    branch_out[...] = last(1)

    for cp in sent:
        cp.wait_send()
    for k in kinds:
        for dz in range(1, O):
            i = at.index(-dz, 0, 0)
            for dy in range(1, I):
                y_copy(k, dy, dz, i).wait_send()
            third_copy(k, dz).wait_send()
        for dy in range(I):
            for dz in range(O):
                if C > 1:
                    if dy + dz > 0:
                        c_copy(k, dy * O + dz, at.index(-dz, -dy, 0)).wait_send()
                    mate_copy(k, dy * O + dz).wait_send()
                if dy > 0:
                    second_copy(k, dy, dz).wait_send()
    for dr in range(1, rows):
        row_copy(dr, row).wait_send()


def shards(rows, cols, q, o, g, log_norm, leaf, root, branch, lens, seg, segb):
    O, I, C = split_cols(cols)
    slots = O * I
    tok = q.shape[0]
    n = tok * HEADS
    rb, kw = root.shape
    nb, bb, _ = branch.shape
    rest = max(slots - O, 1)
    rim = max(O - 1, 1)
    dma = pltpu.SemaphoreType.DMA
    V = pltpu.VMEM
    any_ = pl.BlockSpec(memory_space=pl.ANY)
    big = max(KB, tok, rb * C)

    def both(lead, dtype):
        return [V((lead, rb, kw), dtype), V((lead, nb, bb, kw), dtype)]

    return pl.pallas_call(
        functools.partial(fused_kernel, rows, cols),
        out_shape=(
            jax.ShapeDtypeStruct(q.shape, BF16),
            jax.ShapeDtypeStruct(leaf.shape, F32),
            jax.ShapeDtypeStruct(root.shape, F32),
            jax.ShapeDtypeStruct(branch.shape, F32),
        ),
        in_specs=[SMEM] * 2 + [any_] * 3 + [VMEM] + [any_] * 3 + [VMEM],
        out_specs=(VMEM,) * 4,
        scratch_shapes=[
            V(q.shape, BF16), V(q.shape, BF16), V(q.shape, BF16), V(leaf.shape, BF16),
            V((rb * cols, kw), BF16), V((nb, bb * cols, kw), BF16),
            V((rb * cols, kw), F32), V((nb, bb * cols, kw), F32),
            V((HD, n), BF16), V((HD, n), BF16), V((n, HD), BF16), V((n, HD), BF16),
            V((nb * HD, n), BF16), V((nb * HD, n), BF16),
            V((n, nb * HD), BF16), V((n, nb * HD), BF16),
            V((HD, n), F32), V((big, n), BF16), V((big, n), BF16),
            V((HEADS, tok), F32), V((HEADS, tok), F32),
            *both(slots, F32), *both(O, F32), *both(rest, BF16), *both(rest, BF16),
            *both(rim, BF16), *both(rim, BF16), V((rows, rb, kw), F32),
            dma((6,)), dma((O, 2)), dma((O, 2)),
            *[dma((slots, 2)) for _ in range(8)],
            dma((O, 2)), dma((O, 2)), dma((rows,)), dma((rows,)),
        ],
        compiler_params=pltpu.CompilerParams(
            collective_id=0, has_side_effects=True, vmem_limit_bytes=56 << 20
        ),
        name="fused_grads",
    )(lens, segb, q, o, g, log_norm.T, leaf, root, branch, seg)


def solution(mesh):
    both = P(("rows", "cols"), None)
    in_specs = (
        both, both, both, both, both, P("cols", None), P("rows", "cols", None), P(), both, both,
    )
    out_specs = (both, both, P("cols", None), P("rows", "cols", None))
    body = functools.partial(shards, mesh.shape["rows"], mesh.shape["cols"])
    return jax.shard_map(body, mesh=mesh, in_specs=in_specs, out_specs=out_specs, check_vma=False)
```
